32 devices in a mesh: lat: 16 (over z, y, core), rad: 2 (over x).
Axes of the slice: x: 2, y: 2, z: 4, core: 2. Of those that a mesh axis runs over, the one named last changes fastest.
Arguments:
- displacement: float32 [256, 8, 2048], P('lat', 'rad'), may hold values from -3 to 3
- memory: float32 [256, 8, 2048], P('lat', 'rad'), may hold values from -3 to 3
- ice_class: int32 [256, 2048], P('lat'), may hold values from 0 to 7
- material: int32 [256, 8], P('lat', 'rad'), may hold values from 0 to 7
- mu_table: float32 [8], replicated, may hold values from 0.5 to 4
- decay_table: float32 [8], replicated, may hold values from 0.2 to 0.95
- contrast_table: float32 [8], replicated, may hold values from 0.5 to 2
- gravity_kernel: float32 [256, 8, 8], P('lat', 'rad'), may hold values from -2 to 2
Outputs:
- displacement_out: float32 [256, 8, 2048], P('lat', 'rad')
- memory_out: float32 [256, 8, 2048], P('lat', 'rad')
- potential: float32 [256, 8, 2048], P('lat', 'rad')
The draws below stay inside these ranges and needn't reach their ends.
All inputs are finite; a program needn't handle non-finite values.
Results may differ from the reference program's by a relative error of at most 0.0028.
Values sent between devices are 32-bit elements; how exact they have to be, the bound alone decides.
A program may use at most 64 MiB of HBM per device.

```python
import math
import jax
import jax.numpy as jnp
from jax import lax

NLON = 2048
MODES = 256
NDEG = 256
NMAT = 8
NCLASS = 8
NLAT = 256
NR = 8


def place_ends(entries, rng, least, top_value):
    spot = [jax.random.randint(jax.random.fold_in(rng, axis), (), 0, length) for axis, length in enumerate(entries.shape)]
    main_axis = entries.shape.index(max(entries.shape))
    neighbour = spot[:main_axis] + [(spot[main_axis] + 1) % entries.shape[main_axis]] + spot[main_axis + 1:]
    return entries.at[tuple(spot)].set(least).at[tuple(neighbour)].set(top_value)


def block_scale(rng, extent, cuts, low, high):
    factor_of, own = 1.0, jax.random.fold_in(rng, 6)
    for position, blocks in cuts:
        draws = jnp.exp(jax.random.uniform(jax.random.fold_in(own, position), (blocks,), jnp.float32, low / len(cuts), high / len(cuts)))
        factor_of = factor_of * jnp.repeat(draws, extent[position] // blocks).reshape([-1 if axis == position else 1 for axis in range(len(extent))])
    return factor_of


def centred(rng, shape, deviation, limit, pieces=(), held_as=jnp.bfloat16):
    values = jax.random.normal(rng, shape, jnp.float32) * deviation
    if len(pieces) > 0:
        values = block_scale(rng, shape, pieces, -0.22, 0.18) * values
    return jnp.clip(values, min=-limit, max=limit).astype(held_as)


def setup_inputs(seed: int = 0) -> dict:
    keys = jax.random.split(jax.random.key(seed), 9)
    return {
        "displacement": centred(keys[0], (NLAT, NR, NLON), 0.5, 3.0, ((0, 16), (1, 2)), jnp.float32),
        "memory": centred(keys[1], (NLAT, NR, NLON), 0.5, 3.0, ((0, 16), (1, 2)), jnp.float32),
        "ice_class": place_ends(jax.random.randint(keys[2], (NLAT, NLON), 0, NCLASS), jax.random.fold_in(keys[2], 1), 0, NCLASS - 1).astype(jnp.int32),
        "material": place_ends(jax.random.randint(keys[3], (NLAT, NR), 0, NMAT), jax.random.fold_in(keys[3], 1), 0, NMAT - 1).astype(jnp.int32),
        "mu_table": jnp.clip(jnp.exp(jax.random.uniform(keys[4], (NMAT,), jnp.float32, math.log(0.5), math.log(4.0))), 0.5, 4.0),
        "decay_table": jnp.clip(jax.random.uniform(keys[5], (NMAT,), jnp.float32, 0.2, 0.95), 0.2, 0.95),
        "contrast_table": jnp.clip(jax.random.uniform(keys[6], (NMAT,), jnp.float32, 0.5, 2.0), 0.5, 2.0),
        "gravity_kernel": centred(keys[7], (NDEG, NR, NR), NR ** -0.5, 2.0, ((0, 16), (1, 2)), jnp.float32),
    }


load_scale = 0.5
kappa_shift = 0.5
relax_factor = 0.8
coupling = 2.0

def lookup(material, table):
    onehot = (material[:, :, None] == jnp.arange(table.shape[0], dtype=jnp.int32)[None, None, :]).astype(jnp.float32)
    return lax.optimization_barrier(jnp.sum(onehot * table[None, None, :], axis=-1))

def fourier_table(nlon, modes):
    longitude = jnp.arange(nlon, dtype=jnp.int32)
    order = jnp.arange(modes, dtype=jnp.int32)
    phase = (longitude[:, None] * order[None, :] % nlon).astype(jnp.float32)
    angle = phase * (2.0 * jnp.pi / nlon)
    scale = jnp.sqrt(jnp.float32(2.0) / nlon)
    return scale * jnp.concatenate([jnp.cos(angle), jnp.sin(angle)], axis=1)

def legendre(cosine, count):

    def step(carry, degree):
        before, current = carry
        nextone = ((2.0 * degree + 1.0) * cosine * current - degree * before) / (degree + 1.0)
        return ((current, nextone), current * jnp.sqrt(degree + 0.5))
    start = (jnp.zeros_like(cosine), jnp.ones_like(cosine))
    _, rows = lax.scan(step, start, jnp.arange(count, dtype=jnp.float32))
    return rows

def sweep(field, memory, source, stiff, decay):
    padded = jnp.pad(field, ((1, 1), (1, 1), (0, 0)))
    beside = padded[2:, 1:-1] + padded[:-2, 1:-1] + padded[1:-1, 2:] + padded[1:-1, :-2]
    beside = beside + jnp.roll(field, 1, axis=2) + jnp.roll(field, -1, axis=2)
    diagonal = stiff * (6.0 + kappa_shift)
    applied = diagonal * field - stiff * beside
    update = relax_factor * (source - memory - applied) / diagonal
    return (field + update, decay * memory + stiff * update)

def reference(displacement, memory, ice_class, material, mu_table, decay_table, contrast_table, gravity_kernel):
    stiff = lookup(material, mu_table)[:, :, None]
    decay = lookup(material, decay_table)[:, :, None]
    contrast = lookup(material, contrast_table)[:, :, None]
    layer_pos = (jnp.arange(NR, dtype=jnp.float32) + 1.0) / NR
    source = load_scale * ice_class.astype(jnp.float32)[:, None, :] * layer_pos[None, :, None]
    field, mem = (displacement, memory)
    for step in range(3):
        field, mem = sweep(field, mem, source, stiff, decay)
    rho = contrast * field
    rho = rho - jnp.sum(rho) / (NLAT * NR * NLON)
    table = fourier_table(NLON, MODES)
    cols = 2 * MODES
    spectra = jnp.dot(rho.reshape(NLAT * NR, NLON), table, precision=lax.Precision.HIGHEST).reshape(NLAT, NR * cols)
    theta = (jnp.arange(NLAT, dtype=jnp.float32) + 0.5) * (jnp.pi / NLAT)
    basis = legendre(jnp.cos(theta), NDEG)
    weighted = basis * (jnp.pi / NLAT * jnp.sin(theta))[None, :]
    coef = jnp.dot(weighted, spectra, precision=lax.Precision.HIGHEST).reshape(NDEG, NR, cols)
    phi = jnp.einsum('nab,nbk->nak', gravity_kernel, coef, precision=lax.Precision.HIGHEST)
    synth = jnp.dot(basis.T, phi.reshape(NDEG, NR * cols), precision=lax.Precision.HIGHEST)
    potential = jnp.dot(synth.reshape(NLAT * NR, cols), table.T, precision=lax.Precision.HIGHEST).reshape(NLAT, NR, NLON)
    loaded = source + coupling * potential
    for step in range(3):
        field, mem = sweep(field, mem, loaded, stiff, decay)
    return (field, mem, potential)
```

```python
import jax
import jax.numpy as jnp
import numpy as np
from jax import lax
from jax.sharding import PartitionSpec as P

MODES = 256


load_scale = 0.5
kappa_shift = 0.5
relax_factor = 0.8
coupling = 2.0
HIGH = lax.Precision.HIGH


def lookup(material, table):
    onehot = (
        material[:, :, None] == jnp.arange(table.shape[0], dtype=jnp.int32)[None, None, :]
    ).astype(jnp.float32)
    return jnp.sum(onehot * table[None, None, :], axis=-1)


def fourier_parts(nlon, modes, minor=128):
    order = np.arange(modes)
    parts = []
    for place in (np.arange(nlon // minor) * minor, np.arange(minor)):
        angle = (place[:, None] * order[None, :] % nlon) * (2.0 * np.pi / nlon)
        parts += [np.cos(angle), np.sin(angle)]
    scale = np.sqrt(2.0 / nlon)
    return [(part * f).astype(np.float32) for part, f in zip(parts, (scale, scale, 1.0, 1.0))]


def fourier_table(nlon, modes):
    ca, sa, cb, sb = lax.optimization_barrier([jnp.asarray(p) for p in fourier_parts(nlon, modes)])
    ca, sa, cb, sb = ca[:, None], sa[:, None], cb[None], sb[None]
    cos = (ca * cb - sa * sb).reshape(nlon, modes)
    sin = (sa * cb + ca * sb).reshape(nlon, modes)
    return jnp.concatenate([cos, sin], axis=1)


def legendre(lat, degrees):
    theta = np.pi * (np.arange(lat) + 0.5) / lat
    cosine = np.cos(theta)
    before, current, rows = np.zeros(lat), np.ones(lat), []
    for n in range(degrees):
        rows.append(current * np.sqrt(n + 0.5))
        before, current = current, ((2.0 * n + 1.0) * cosine * current - n * before) / (n + 1.0)
    basis = np.stack(rows)
    weighted = basis * (np.pi / lat * np.sin(theta))[None, :]
    return basis, weighted


def neighbours(x, axis, dim):
    devices, length = (lax.axis_size(axis), x.shape[dim])
    up = [(i, i + 1) for i in range(devices - 1)]
    down = [(j, i) for i, j in up]
    last = lax.slice_in_dim(x, length - 1, length, axis=dim)
    first = lax.slice_in_dim(x, 0, 1, axis=dim)
    return lax.ppermute(last, axis, up), lax.ppermute(first, axis, down)


def sweep(field, memory, source, stiff, decay):
    beside = jnp.roll(field, 1, axis=2) + jnp.roll(field, -1, axis=2)
    for axis, dim in (("lat", 0), ("rad", 1)):
        length = field.shape[dim]
        before, after = neighbours(field, axis, dim)
        beside = beside + jnp.concatenate(
            [before, lax.slice_in_dim(field, 0, length - 1, axis=dim)], axis=dim
        )
        beside = beside + jnp.concatenate(
            [lax.slice_in_dim(field, 1, length, axis=dim), after], axis=dim
        )
    diagonal = 6.0 + kappa_shift
    update = relax_factor * (
        (source - memory) * (1.0 / (stiff * diagonal)) - field + beside * (1.0 / diagonal)
    )
    return (field + update, decay * memory + stiff * update)


def per_device(
    displacement, memory, ice_class, material, mu_table, decay_table, contrast_table, gravity_kernel
):
    lat_dev, r_dev, nlon = displacement.shape
    lat_count = lax.axis_size("lat")
    rad_count = lax.axis_size("rad")
    rad_index = lax.axis_index("rad")
    total_lat = lat_count * lat_dev
    total_rad = rad_count * r_dev
    degrees = gravity_kernel.shape[0] * lat_count
    cols = 2 * MODES
    columns = cols // lat_count
    kernel_every = lax.all_gather(gravity_kernel, "lat", axis=0, tiled=True)
    stiff = lookup(material, mu_table)[:, :, None]
    decay = lookup(material, decay_table)[:, :, None]
    contrast = lookup(material, contrast_table)[:, :, None]
    layer_pos = (rad_index * r_dev + jnp.arange(r_dev, dtype=jnp.int32) + 1).astype(
        jnp.float32
    ) / total_rad
    source = load_scale * ice_class.astype(jnp.float32)[:, None, :] * layer_pos[None, :, None]
    basis, weighted = legendre(total_lat, degrees)
    projection = jnp.asarray(
        np.concatenate([weighted, np.ones((8, total_lat))]).astype(np.float32)
    )
    weight_sum = jnp.asarray(weighted.sum(axis=1).astype(np.float32))
    basis = jnp.asarray(basis.T.astype(np.float32))
    table = fourier_table(nlon, MODES)
    field, mem = (displacement, memory)
    for step in range(3):
        field, mem = sweep(field, mem, source, stiff, decay)
    rho = contrast * field
    spectra = jnp.dot(rho.reshape(lat_dev * r_dev, nlon), table, precision=HIGH)
    spread = lax.all_to_all(
        spectra.reshape(lat_dev, r_dev, cols), "lat", split_axis=2, concat_axis=0, tiled=True
    )
    coef_cols = jnp.dot(
        projection, spread.reshape(total_lat, r_dev * columns), precision=HIGH
    ).reshape(degrees + 8, r_dev, columns)
    coef_all = lax.all_gather(coef_cols, "rad", axis=1, tiled=True)
    first_order = (lax.axis_index("lat") * columns + jnp.arange(columns, dtype=jnp.int32)) == 0
    mean_row = jnp.sum(coef_all[degrees], axis=0) / (total_lat * total_rad)
    mean_row = jnp.where(first_order, mean_row, 0.0)
    coef_all = coef_all[:degrees] - weight_sum[:, None, None] * mean_row[None, None, :]
    phi_cols = jnp.sum(kernel_every[:, :, :, None] * coef_all[:, None, :, :], axis=2)
    synth_cols = jnp.dot(
        basis, phi_cols.reshape(degrees, r_dev * columns), precision=HIGH
    ).reshape(total_lat, r_dev, columns)
    synth = lax.all_to_all(synth_cols, "lat", split_axis=0, concat_axis=2, tiled=True)
    potential = lax.dot_general(
        synth.reshape(lat_dev * r_dev, cols), table, (((1,), (1,)), ((), ())), precision=HIGH
    ).reshape(lat_dev, r_dev, nlon)
    loaded = source + coupling * potential
    for step in range(3):
        field, mem = sweep(field, mem, loaded, stiff, decay)
    return (field, mem, potential)


def solution(mesh):
    placed = (
        P("lat", "rad", None),
        P("lat", "rad", None),
        P("lat", None),
        P("lat", "rad"),
        P(),
        P(),
        P(),
        P("lat", "rad", None),
    )
    return jax.shard_map(
        per_device,
        mesh=mesh,
        in_specs=placed,
        out_specs=(P("lat", "rad", None), P("lat", "rad", None), P("lat", "rad", None)),
        check_vma=False,
    )
```

```python
import jax
import jax.numpy as jnp
import numpy as np
from jax import lax
from jax.experimental import pallas as pl
from jax.experimental.pallas import tpu as pltpu
from jax.sharding import PartitionSpec as P

MODES = 256


load_scale = 0.5
kappa_shift = 0.5
relax_factor = 0.8
coupling = 2.0
HIGH = lax.Precision.HIGH


def lookup(material, table):
    onehot = (
        material[:, :, None] == jnp.arange(table.shape[0], dtype=jnp.int32)[None, None, :]
    ).astype(jnp.float32)
    return jnp.sum(onehot * table[None, None, :], axis=-1)


def fourier_parts(nlon, modes, minor=128):
    order = np.arange(modes)
    parts = []
    for place in (np.arange(nlon // minor) * minor, np.arange(minor)):
        angle = (place[:, None] * order[None, :] % nlon) * (2.0 * np.pi / nlon)
        parts += [np.cos(angle), np.sin(angle)]
    scale = np.sqrt(2.0 / nlon)
    return [(part * f).astype(np.float32) for part, f in zip(parts, (scale, scale, 1.0, 1.0))]


def fourier_table(nlon, modes):
    ca, sa, cb, sb = lax.optimization_barrier([jnp.asarray(p) for p in fourier_parts(nlon, modes)])
    ca, sa, cb, sb = ca[:, None], sa[:, None], cb[None], sb[None]
    cos = (ca * cb - sa * sb).reshape(nlon, modes)
    sin = (sa * cb + ca * sb).reshape(nlon, modes)
    return jnp.concatenate([cos, sin], axis=1)


def legendre(lat, degrees):
    theta = np.pi * (np.arange(lat) + 0.5) / lat
    cosine = np.cos(theta)
    before, current, rows = np.zeros(lat), np.ones(lat), []
    for n in range(degrees):
        rows.append(current * np.sqrt(n + 0.5))
        before, current = current, ((2.0 * n + 1.0) * cosine * current - n * before) / (n + 1.0)
    basis = np.stack(rows)
    weighted = basis * (np.pi / lat * np.sin(theta))[None, :]
    return basis, weighted


def sweeps_kernel(steps, gather, *refs):
    if gather:
        f_ref, m_ref, s_ref, stiff_ref, decay_ref, g_ref, f_out, m_out, g_out, *refs = refs
        f_buf, face, lat_in, rad_in, send, recv, g_in, g_send, g_recv = refs
    else:
        f_ref, m_ref, s_ref, stiff_ref, decay_ref, f_out, m_out, *refs = refs
        f_buf, face, lat_in, rad_in, send, recv = refs
    layers, rows, nlon = f_ref.shape
    lat_n, rad_n = lax.axis_size("lat"), lax.axis_size("rad")
    lat, rad = lax.axis_index("lat"), lax.axis_index("rad")
    north = (lax.rem(lat + lat_n - 1, lat_n), rad)
    south = (lax.rem(lat + 1, lat_n), rad)
    below = (lat, lax.rem(rad + rad_n - 1, rad_n))
    above = (lat, lax.rem(rad + 1, rad_n))
    if gather:
        peers = [(lax.rem(lat + d, lat_n), rad) for d in range(1, lat_n)] + [below, above]
    else:
        peers = [north, south, below, above]
    barrier = pltpu.get_barrier_semaphore()
    for peer in peers:
        pl.semaphore_signal(barrier, inc=1, device_id=peer, device_id_type=pl.DeviceIdType.MESH)
    pl.semaphore_wait(barrier, len(peers))

    def remote(src, dst, send_sem, recv_sem, peer):
        copy = pltpu.make_async_remote_copy(
            src_ref=src, dst_ref=dst, send_sem=send_sem, recv_sem=recv_sem,
            device_id=peer, device_id_type=pl.DeviceIdType.MESH,
        )
        copy.start()
        return copy

    weight = relax_factor / (6.0 + kappa_shift)
    w_north = jnp.where(lat > 0, weight, 0.0)
    w_south = jnp.where(lat < lat_n - 1, weight, 0.0)
    w_below = jnp.where(rad > 0, weight, 0.0)
    w_above = jnp.where(rad < rad_n - 1, weight, 0.0)
    row = lax.broadcasted_iota(jnp.int32, (rows, nlon), 0)
    gathered = []
    for step in range(steps):
        old = f_ref if step == 0 else f_buf.at[step - 1]
        new = f_out if step == steps - 1 else f_buf.at[step]
        old_m = m_ref if step == 0 else m_out
        for r in range(layers):
            face[step, 0, r : r + 1, :] = old[r, 0:1, :]
            face[step, 1, r : r + 1, :] = old[r, rows - 1 : rows, :]
        copies = [
            remote(old.at[0], rad_in.at[step, 1], send.at[step, 0], recv.at[step, 0], below),
            remote(old.at[layers - 1], rad_in.at[step, 0], send.at[step, 1], recv.at[step, 1], above),
            remote(face.at[step, 0], lat_in.at[step, 1], send.at[step, 2], recv.at[step, 2], north),
            remote(face.at[step, 1], lat_in.at[step, 0], send.at[step, 3], recv.at[step, 3], south),
        ]
        if gather and step == 0:
            gathered = [
                remote(g_ref, g_in.at[lat], g_send.at[d], g_recv.at[d], peers[d - 1])
                for d in range(1, lat_n)
            ]
        for r in range(layers):
            f, m = old[r], old_m[r]
            beside = pltpu.roll(f, 1, 1) + pltpu.roll(f, nlon - 1, 1)
            beside += jnp.where(row == 0, 0.0, pltpu.roll(f, 1, 0))
            beside += jnp.where(row == rows - 1, 0.0, pltpu.roll(f, rows - 1, 0))
            if r > 0:
                beside += old[r - 1]
            if r < layers - 1:
                beside += old[r + 1]
            stiff = stiff_ref[r]
            update = (s_ref[r] - m) * (weight / stiff) - relax_factor * f + weight * beside
            new[r] = f + update
            m_out[r] = decay_ref[r] * m + stiff * update
        for copy in copies:
            copy.wait()
        for r, slot, w in ((0, 0, w_below), (layers - 1, 1, w_above)):
            extra = w * rad_in[step, slot]
            new[r] += extra
            m_out[r] += stiff_ref[r] * extra
        for r in range(layers):
            for j, slot, w in ((0, 0, w_north), (rows - 1, 1, w_south)):
                extra = w * lat_in[step, slot, r : r + 1, :]
                new[r, j : j + 1, :] += extra
                m_out[r, j : j + 1, :] += stiff_ref[r, j : j + 1, :] * extra
    if gather:
        for copy in gathered:
            copy.wait()
        g_in[lat] = g_ref[...]
        g_out[...] = g_in[...]


def sweeps(steps, field, memory, source, stiff, decay, gravity=None):
    gather = gravity is not None
    layers, rows, nlon = field.shape
    block = jax.ShapeDtypeStruct(field.shape, jnp.float32)
    operands, out = [field, memory, source, stiff, decay], [block, block]
    dma, f32 = pltpu.SemaphoreType.DMA, jnp.float32
    scratch = [
        pltpu.VMEM((steps - 1, layers, rows, nlon), f32),
        pltpu.VMEM((steps, 2, layers, nlon), f32),
        pltpu.VMEM((steps, 2, layers, nlon), f32),
        pltpu.VMEM((steps, 2, rows, nlon), f32),
        dma((steps, 4)),
        dma((steps, 4)),
    ]
    if gather:
        lat_n = lax.axis_size("lat")
        every = (lat_n,) + gravity.shape
        operands.append(gravity)
        out.append(jax.ShapeDtypeStruct(every, f32))
        scratch += [pltpu.VMEM(every, f32), dma((lat_n,)), dma((lat_n,))]
    vmem = pl.BlockSpec(memory_space=pltpu.VMEM)

    def kernel(*refs):
        sweeps_kernel(steps, gather, *refs)

    return pl.pallas_call(
        kernel,
        out_shape=out,
        in_specs=[vmem] * len(operands),
        out_specs=[vmem] * len(out),
        scratch_shapes=scratch,
        compiler_params=pltpu.CompilerParams(
            collective_id=0 if gather else 1, has_side_effects=True
        ),
    )(*operands)


def per_device(
    displacement, memory, ice_class, material, mu_table, decay_table, contrast_table, gravity_kernel
):
    lat_dev, r_dev, nlon = displacement.shape
    lat_count = lax.axis_size("lat")
    rad_count = lax.axis_size("rad")
    rad_index = lax.axis_index("rad")
    total_lat = lat_count * lat_dev
    total_rad = rad_count * r_dev
    degrees = gravity_kernel.shape[0] * lat_count
    cols = 2 * MODES
    columns = cols // lat_count
    stiff = lookup(material.T, mu_table)[:, :, None]
    decay = lookup(material.T, decay_table)[:, :, None]
    contrast = lookup(material.T, contrast_table)[:, :, None]
    layer_pos = (rad_index * r_dev + jnp.arange(r_dev, dtype=jnp.int32) + 1).astype(
        jnp.float32
    ) / total_rad
    source = load_scale * ice_class.astype(jnp.float32)[None, :, :] * layer_pos[:, None, None]
    basis, weighted = legendre(total_lat, degrees)
    projection = jnp.asarray(
        np.concatenate([weighted, np.ones((8, total_lat))]).astype(np.float32)
    )
    weight_sum = jnp.asarray(weighted.sum(axis=1).astype(np.float32))
    basis = jnp.asarray(basis.T.astype(np.float32))
    table = fourier_table(nlon, MODES)
    field, mem, kernel_every = sweeps(
        3,
        displacement.transpose(1, 0, 2),
        memory.transpose(1, 0, 2),
        source,
        stiff,
        decay,
        gravity_kernel.reshape(gravity_kernel.shape[0], -1),
    )
    kernel_every = kernel_every.reshape((degrees,) + gravity_kernel.shape[1:])
    rho = contrast * field
    spectra = jnp.dot(rho.reshape(lat_dev * r_dev, nlon), table, precision=HIGH)
    spread = lax.all_to_all(
        spectra.reshape(r_dev, lat_dev, cols).transpose(1, 0, 2), "lat", split_axis=2, concat_axis=0, tiled=True
    )
    coef_cols = jnp.dot(
        projection, spread.reshape(total_lat, r_dev * columns), precision=HIGH
    ).reshape(degrees + 8, r_dev, columns)
    coef_all = lax.all_gather(coef_cols, "rad", axis=1, tiled=True)
    first_order = (lax.axis_index("lat") * columns + jnp.arange(columns, dtype=jnp.int32)) == 0
    mean_row = jnp.sum(coef_all[degrees], axis=0) / (total_lat * total_rad)
    mean_row = jnp.where(first_order, mean_row, 0.0)
    coef_all = coef_all[:degrees] - weight_sum[:, None, None] * mean_row[None, None, :]
    phi_cols = jnp.sum(kernel_every[:, :, :, None] * coef_all[:, None, :, :], axis=2)
    synth_cols = jnp.dot(
        basis, phi_cols.reshape(degrees, r_dev * columns), precision=HIGH
    ).reshape(total_lat, r_dev, columns)
    synth = lax.all_to_all(synth_cols, "lat", split_axis=0, concat_axis=2, tiled=True)
    potential = lax.dot_general(
        synth.transpose(1, 0, 2).reshape(r_dev * lat_dev, cols), table, (((1,), (1,)), ((), ())), precision=HIGH
    ).reshape(r_dev, lat_dev, nlon)
    loaded = source + coupling * potential
    field, mem = sweeps(3, field, mem, loaded, stiff, decay)
    return tuple(x.transpose(1, 0, 2) for x in (field, mem, potential))


def solution(mesh):
    placed = (
        P("lat", "rad", None),
        P("lat", "rad", None),
        P("lat", None),
        P("lat", "rad"),
        P(),
        P(),
        P(),
        P("lat", "rad", None),
    )
    return jax.shard_map(
        per_device,
        mesh=mesh,
        in_specs=placed,
        out_specs=(P("lat", "rad", None), P("lat", "rad", None), P("lat", "rad", None)),
        check_vma=False,
    )
```
